512 devices in a mesh: dp: 4 (over y), frames: 16 (over z), height: 8 (over x, core).
Axes of the slice: x: 4, y: 4, z: 16, core: 2. Of those that a mesh axis runs over, the one named last changes fastest.
Arguments:
- video: bfloat16 [512, 8, 16, 640], P(('dp', 'frames'), 'height'), parts along dimension 0
- window_gaps: int32 [112], P('dp'), parts along dimension 0, may hold values from 1 to 8, 112 in all
- gn_gain: float32 [640], replicated, may hold values from 0.25 to 1.75
- gn_bias: float32 [640], replicated, may hold values from -3 to 3
- conv_weight: bfloat16 [5760, 640], P('frames', 'height'), may hold values from -0.078125 to 0.078125
- conv_bias: float32 [640], replicated, may hold values from -3 to 3
- ln_gain: float32 [640], replicated, may hold values from 0.25 to 1.75
- ln_bias: float32 [640], replicated, may hold values from -3 to 3
- qkv_weight: bfloat16 [640, 1920], replicated, may hold values from -0.25 to 0.25
- out_weight: bfloat16 [640, 640], replicated, may hold values from -0.5 to 0.5
- out_bias: float32 [640], replicated, may hold values from -3 to 3
Outputs:
- output: bfloat16 [512, 8, 16, 640], P(('dp', 'frames'), 'height'), parts along dimension 0
The draws below stay inside these ranges and needn't reach their ends.
There are 4 independent parts, one for each index of `dp`. The reference program is written for one: setup_inputs(seed, part) draws one part's arguments, and reference() takes and returns one part's arrays. A program takes and returns all parts, laid end to end along the dimension named above; an argument that names none is the same for every part. Nothing has to cross between parts.
Inputs may be any that keep to these rules, and one draw needn't show every extreme that they name: `window_gaps`: the first window starts at frame 0 and the last at 112; the largest gap 16 // 2 is reached in every draw.
All inputs are finite; a program needn't handle non-finite values.
Results may differ from the reference program's by a relative error of at most 0.008.
Values may be sent and summed in bfloat16 or wider, within the bound.
No kernel may reach another device: no remote copies, remote signals or barrier semaphores. Data moves between devices by JAX's collectives and lax.ppermute only.
A program may use at most 64 MiB of HBM per device.

```python
import math
import jax
import jax.numpy as jnp
import numpy as np
from jax import lax

C = 640
HEADS = 10
GROUPS = 32
WIN = 16
ROW_W = 16
HEAD_DIM = 64
FRAMES = 128
H = 8
NWIN = 29


def draw_video(key, part):
    key_base = jax.random.fold_in(key, 0)
    key_jitter = jax.random.fold_in(key, 1)
    key_chan = jax.random.fold_in(key, 2)
    key_sign = jax.random.fold_in(key, 4)
    key_level = jax.random.fold_in(key, 5)
    base = jax.random.normal(key_base, (FRAMES, H, ROW_W, C), jnp.float32)
    rising = 0.3 * 3.0 ** (jnp.arange(H, dtype=jnp.float32) / max(H - 1, 1))
    jitter = jnp.exp(jax.random.uniform(key_jitter, (FRAMES, H, 1, 1), jnp.float32, 0.0, 0.7))
    channel_scale = jnp.exp(jax.random.uniform(key_chan, (1, 1, 1, C), jnp.float32, -0.4, 0.4))
    values = base * rising[None, :, None, None] * jitter * channel_scale
    signs = jnp.where(jax.random.uniform(key_sign, (FRAMES, 1, 1, GROUPS, 1), jnp.float32) < 0.5, -1.0, 1.0)
    level = jax.random.uniform(key_level, (FRAMES, 1, 1, GROUPS, 1), jnp.float32, 0.6, 1.4)
    band_level = 0.4 * 3.0 ** (jnp.arange(H, dtype=jnp.float32) / max(H - 1, 1))
    offset = signs * level * band_level[None, :, None, None, None]
    offset = jnp.broadcast_to(offset, (FRAMES, H, ROW_W, GROUPS, C // GROUPS)).reshape(FRAMES, H, ROW_W, C)
    values = values + offset
    return values.astype(jnp.bfloat16)


def block_scale(stream_key, extent, shards, least, largest):
    def one(position, parts):
        steps = jax.random.uniform(jax.random.fold_in(jax.random.fold_in(stream_key, 6), position), (parts,), jnp.float32, least / len(shards), largest / len(shards))
        return jnp.repeat(jnp.exp(steps), extent[position] // parts).reshape((-1,) + (1,) * (len(extent) - position - 1))

    level = one(*shards[0])
    for cut in shards[1:]:
        level = level * one(*cut)
    return level


def profile(amount, total, bound, skew):
    weights = [(1 << 20) // math.isqrt(grade ** skew) + 1 for grade in range(2, amount + 1)]
    spare, counts = total - bound - (amount - 1), [1] * (amount - 1)
    while spare > 0:
        free = [i for i in range(amount - 1) if counts[i] < bound]
        pool, budget = sum([weights[i] for i in free]), spare
        for i in free:
            addition = min(bound - counts[i], max(1, budget * weights[i] // pool), spare)
            counts[i] = counts[i] + addition
            spare = spare - addition
    return np.array([bound] + counts)


def uneven(rng, number_of, total, most, slope):
    if number_of == 2:
        one = jax.random.randint(rng, (), max(1, total - most), min(most, total - 1) + 1)
        return jnp.stack([one, total - one])
    lengths = jnp.asarray(profile(number_of, total, most, slope), jnp.int32)
    couples = (number_of - 1) // 2
    giver, taker = lengths[1:1 + 2 * couples:2], lengths[2:2 + 2 * couples:2]
    room = jnp.minimum(giver - 1, most - taker)
    shifted = jax.random.randint(jax.random.fold_in(rng, 1), (couples,), 0, 1 << 20) % (room + 1)
    lengths = lengths.at[1:1 + 2 * couples:2].set(giver - shifted).at[2:2 + 2 * couples:2].set(taker + shifted)
    return lengths[jax.random.permutation(jax.random.fold_in(rng, 2), number_of)]


def centred(rng, shape, width, bound, shards=(), kind=jnp.bfloat16):
    entries = width * jax.random.normal(rng, shape, jnp.float32)
    if shards:
        entries = entries * block_scale(rng, shape, shards, -0.22, 0.18)
    return jnp.clip(entries, -bound, bound).astype(kind)


def setup_inputs(seed: int = 0, part: int = 0) -> dict:
    streams_of = jax.random.split(jax.random.key(seed), 12)
    own_keys = jax.random.split(jax.random.fold_in(streams_of[11], part), 12)
    return {
        "video": draw_video(jax.random.fold_in(jax.random.fold_in(streams_of[11], part), 71), part),
        "window_gaps": uneven(own_keys[1], NWIN - 1, FRAMES - WIN, WIN // 2, 2).astype(jnp.int32),
        "gn_gain": jnp.clip(1.0 + 0.15 * jax.random.normal(streams_of[2], (C,), jnp.float32), 0.25, 1.75),
        "gn_bias": centred(streams_of[3], (C,), 0.3, 3.0, (), jnp.float32),
        "conv_weight": centred(streams_of[4], (9 * C, C), (9 * C) ** -0.5, 0.078125, ((0, 16), (1, 8))),
        "conv_bias": centred(streams_of[5], (C,), 0.3, 3.0, (), jnp.float32),
        "ln_gain": jnp.clip(1.0 + 0.15 * jax.random.normal(streams_of[6], (C,), jnp.float32), 0.25, 1.75),
        "ln_bias": centred(streams_of[7], (C,), 0.3, 3.0, (), jnp.float32),
        "qkv_weight": centred(streams_of[8], (C, 3 * C), C ** -0.5, 0.25),
        "out_weight": centred(streams_of[9], (C, C), (C // 4) ** -0.5, 0.5),
        "out_bias": centred(streams_of[10], (C,), 0.3, 3.0, (), jnp.float32),
    }


EPSILON = 1e-05

def window_member(window_gaps, frame_ids):
    starts = jnp.concatenate([jnp.zeros((1,), jnp.int32), jnp.cumsum(window_gaps).astype(jnp.int32)])
    inside = (frame_ids[None, :] >= starts[:, None]) & (frame_ids[None, :] < starts[:, None] + WIN)
    return inside.astype(jnp.float32)

def reference(video, window_gaps, gn_gain, gn_bias, conv_weight, conv_bias, ln_gain, ln_bias, qkv_weight, out_weight, out_bias):
    floats = video.astype(jnp.float32)
    grouped = floats.reshape(FRAMES, H, ROW_W, GROUPS, C // GROUPS)
    mean = lax.optimization_barrier(jnp.mean(grouped, axis=(1, 2, 4), keepdims=True))
    variance = lax.optimization_barrier(jnp.mean((grouped - mean) ** 2, axis=(1, 2, 4), keepdims=True))
    normed = ((grouped - mean) * lax.rsqrt(variance + EPSILON)).reshape(FRAMES, H, ROW_W, C) * gn_gain + gn_bias
    activated = jax.nn.silu(normed).astype(jnp.bfloat16)
    padded = jnp.pad(activated, ((0, 0), (1, 1), (1, 1), (0, 0)))
    taps = conv_weight.reshape(9, C, C)

    def conv_frame(frame):
        total = jnp.zeros((H * ROW_W, C), jnp.float32)
        for tap in range(9):
            row_off = tap // 3
            col_off = tap % 3
            piece = frame[row_off:row_off + H, col_off:col_off + ROW_W].reshape(H * ROW_W, C)
            total = total + jnp.dot(piece, taps[tap], preferred_element_type=jnp.float32)
        return total.reshape(H, ROW_W, C)
    conv_sum = lax.map(conv_frame, padded)
    conv_out = lax.optimization_barrier((conv_sum + conv_bias).astype(jnp.bfloat16))
    resid_state = (floats + conv_out.astype(jnp.float32)).astype(jnp.bfloat16)
    resid_float = resid_state.astype(jnp.float32)
    centre = lax.optimization_barrier(jnp.mean(resid_float, axis=-1, keepdims=True))
    deviation = resid_float - centre
    spread = lax.optimization_barrier(jnp.mean(deviation * deviation, axis=-1, keepdims=True))
    normalized = (deviation * lax.rsqrt(spread + EPSILON) * ln_gain + ln_bias).astype(jnp.bfloat16)
    cells = H * ROW_W
    project = jnp.dot(normalized.reshape(-1, C), qkv_weight, preferred_element_type=jnp.float32).astype(jnp.bfloat16)
    project = project.reshape(FRAMES, cells, 3 * C)
    query = project[:, :, :C].reshape(FRAMES, cells, HEADS, HEAD_DIM)
    keys_all = project[:, :, C:2 * C].reshape(FRAMES, cells, HEADS, HEAD_DIM).astype(jnp.float32)
    values_all = project[:, :, 2 * C:].reshape(FRAMES, cells, HEADS, HEAD_DIM).astype(jnp.float32)
    member = window_member(window_gaps, jnp.arange(FRAMES, dtype=jnp.int32))
    frame_count = lax.optimization_barrier(jnp.sum(member, axis=0))
    scale = HEAD_DIM ** (-0.5)

    def attend(inputs):
        query_frame, cover, count_here = inputs
        scores = jnp.einsum('shd,mshd->shm', query_frame.astype(jnp.float32), keys_all, precision=lax.Precision.HIGHEST) * scale
        expo = jnp.exp(scores)
        window_sum = jnp.einsum('shm,wm->shw', expo, member, precision=lax.Precision.HIGHEST)
        coef = cover / (count_here * jnp.where(cover > 0, window_sum, 1.0))
        spread_back = jnp.einsum('shw,wm->shm', coef, member, precision=lax.Precision.HIGHEST)
        attn_weight = (expo * spread_back).astype(jnp.bfloat16)
        mixed = jnp.einsum('shm,mshd->shd', attn_weight.astype(jnp.float32), values_all, precision=lax.Precision.HIGHEST)
        return mixed.astype(jnp.bfloat16)
    mixed = lax.map(attend, (query, member.T, frame_count))
    projected = jnp.dot(mixed.reshape(-1, C), out_weight, preferred_element_type=jnp.float32)
    output = resid_float.reshape(-1, C) + projected + out_bias
    return output.astype(jnp.bfloat16).reshape(FRAMES, H, ROW_W, C)
```

```python
import jax
import jax.numpy as jnp
from jax import lax
from jax.experimental import pallas as pl
from jax.experimental.pallas import tpu as pltpu
from jax.sharding import PartitionSpec as P

HEADS = 10
GROUPS = 32
WIN = 16
HEAD_DIM = 64
LANES = 128

EPSILON = 1e-05
F32 = jnp.float32
BF16 = jnp.bfloat16
VMEM = pl.BlockSpec(memory_space=pltpu.VMEM)
SMEM = pl.BlockSpec(memory_space=pltpu.SMEM)
NT = (((1,), (1,)), ((), ()))


def dot(a, b):
    return jnp.dot(a, b, preferred_element_type=F32)


def exact_dot(a, b, dims=(((1,), (0,)), ((), ()))):
    return lax.dot_general(a, b, dims, precision=lax.Precision.HIGHEST, preferred_element_type=F32)


def iota(shape, dim):
    return lax.broadcasted_iota(jnp.int32, shape, dim)


def conv_kernel(
    place_ref, own_ref, left_ref, right_ref, far_ref, weight_ref, other_ref, gain_ref, bias_ref, cbias_ref,
    out_ref, cells, padded, shifted,
):
    frames, rows, width, chans = cells.shape
    chips = rows // 2
    outs = out_ref.shape[-1]
    chip, core = place_ref[0], place_ref[1]
    for ref, back in ((own_ref, 0), (left_ref, 1), (far_ref, 2), (right_ref, 3)):
        row = 2 * lax.rem(chip + chips - back, chips)
        for f in range(frames):
            cells[f, row + core] = ref[0, f]
            cells[f, row + 1 - core] = ref[1, f]
    groups = (iota((chans, LANES), 0).astype(F32) + 0.5) * (GROUPS / chans)
    groups = (jnp.floor(groups) == iota((chans, LANES), 1).astype(F32)).astype(F32)
    count = rows * width * (chans // GROUPS)

    def group_mean(sums):
        per_group = exact_dot(jnp.concatenate(sums + sums, axis=0), groups) / count
        return exact_dot(per_group, groups, NT)

    def frame(f):
        return cells[f].reshape(rows * width, chans).astype(F32)

    mean = group_mean([jnp.sum(frame(f), axis=0, keepdims=True) for f in range(frames)])
    sums = []
    for f in range(frames):
        centred = frame(f) - mean[f : f + 1]
        sums.append(jnp.sum(centred * centred, axis=0, keepdims=True))
    inverse = lax.rsqrt(group_mean(sums) + EPSILON)
    gain, bias = gain_ref[...], bias_ref[...]
    edge = jnp.zeros((width, chans), BF16)
    for f in range(frames):
        padded[f, 0] = edge
        padded[f, rows + 1] = edge
        for r in range(rows):
            normed = (cells[f, r].astype(F32) - mean[f : f + 1]) * inverse[f : f + 1] * gain + bias
            padded[f, r + 1] = (normed / (1.0 + jnp.exp(-normed))).astype(BF16)
    flat = frames * rows * width
    column = lax.rem(iota((flat, 1), 0), width)
    total = None
    for col in (1, 0, 2):
        part = None
        for row in range(3):
            tap = (3 * row + col) * chans
            term = dot(
                padded[:, row : row + rows].reshape(flat, chans),
                jnp.concatenate(
                    [weight_ref[tap : tap + chans], other_ref[tap : tap + chans]], axis=1
                ),
            )
            part = term if part is None else part + term
        if col == 1:
            total = part + cbias_ref[...]
        else:
            shifted[8 : 8 + flat] = part
            moved = shifted[6 + 2 - 1 : 6 + 2 - 1 + flat] if col == 0 else shifted[9 : 9 + flat]
            total = total + jnp.where(column == (0 if col == 0 else width - 1), 0.0, moved)
    result = total.astype(BF16).reshape(frames, rows, width, outs)
    for r in range(rows):
        for f in range(frames):
            out_ref[r, f * width : (f + 1) * width] = result[f, r]


def swap_matrix(frames, width, back):
    cells = frames * width
    near, far = iota((cells, cells), 1 if back else 0), iota((cells, cells), 0 if back else 1)
    same = (lax.div(near, frames) == lax.rem(far, width)) & (
        lax.rem(near, frames) == lax.div(far, width)
    )
    return same.astype(F32).astype(BF16)


def norm_kernel(part_ref, video_ref, gain_ref, bias_ref, resid_ref, norm_ref):
    cells, chans = video_ref.shape
    half = part_ref.shape[2] // 2
    parts = part_ref.shape[0]
    top = [part_ref[s].astype(F32) for s in range(0, parts, 2)]
    low = []
    for s in range(1, parts, 2):
        piece = part_ref[s].astype(F32)
        low += [piece[:, half:], piece[:, :half]]
    conv_out = jnp.concatenate(
        [jnp.concatenate(top, axis=1), jnp.concatenate(low, axis=1)], axis=0
    )
    resid = (video_ref[...].astype(F32) + conv_out).astype(BF16)
    resid_ref[...] = resid
    floats = resid.astype(F32)
    deviation = floats - jnp.mean(floats, axis=-1, keepdims=True)
    spread = jnp.mean(deviation * deviation, axis=-1, keepdims=True)
    norm = (deviation * lax.rsqrt(spread + EPSILON) * gain_ref[...] + bias_ref[...]).astype(BF16)
    norm_ref[...] = dot(swap_matrix(8, cells // 8, False), norm).astype(BF16)


def attend_kernel(
    b0_ref, b1_ref, b2_ref, b3_ref, b4_ref, resid_ref, qkv_ref, out_w_ref, out_b_ref,
    member_ref, cover_ref,
    out_ref, keys, values, query, scores, mixed,
):
    blocks, width, frames, chans = keys.shape
    near = blocks * frames
    stack = HEADS * frames

    def by_cell(product):
        return product.astype(BF16).astype(F32).reshape(width, frames, chans)

    query[...] = by_cell(dot(b2_ref[...], qkv_ref[:, :chans]))
    for b, ref in enumerate((b0_ref, b1_ref, b2_ref, b3_ref, b4_ref)):
        keys[b] = by_cell(dot(ref[...], qkv_ref[:, chans : 2 * chans]))
        values[b] = by_cell(dot(ref[...], qkv_ref[:, 2 * chans :]))
    head_of = lax.div(iota((HEADS, 1, chans), 2), HEAD_DIM) == iota((HEADS, 1, chans), 0)
    own = head_of.astype(F32)
    for c in range(width):
        spread = (query[c][None] * own).reshape(stack, chans).astype(BF16)
        key = keys[:, c].reshape(near, chans).astype(BF16)
        scores[c] = lax.dot_general(spread, key, NT, preferred_element_type=F32)
    flat = width * stack
    expo = jnp.exp(scores[...].reshape(flat, near) * HEAD_DIM ** (-0.5))
    member = member_ref[...].astype(BF16)

    def split_dot(a, dims):
        high = a.astype(BF16)
        rest = (a - high.astype(F32)).astype(BF16)
        return lax.dot_general(high, member, dims, preferred_element_type=F32) + lax.dot_general(
            rest, member, dims, preferred_element_type=F32
        )

    sums = split_dot(expo, NT).reshape(width * HEADS, frames, LANES)
    cover = cover_ref[...][None]
    frame_count = jnp.sum(cover, axis=2, keepdims=True)
    coef = (cover / (frame_count * jnp.where(cover > 0, sums, 1.0))).reshape(flat, LANES)
    back = split_dot(coef, (((1,), (0,)), ((), ())))
    scores[...] = (expo * back).reshape(width, stack, near)
    for c in range(width):
        value = values[:, c].reshape(near, chans).astype(BF16)
        product = dot(scores[c].astype(BF16), value).reshape(HEADS, frames, chans)
        mixed[c] = jnp.sum(jnp.where(head_of, product, 0.0), axis=0)
    joined = mixed[...].reshape(width * frames, chans).astype(BF16)
    joined = dot(swap_matrix(frames, width, True), joined).astype(BF16)
    projected = dot(joined, out_w_ref[...])
    out_ref[...] = (resid_ref[...].astype(F32) + projected + out_b_ref[...]).astype(BF16)


def passed(shard, axis, by):
    size = lax.axis_size(axis)
    pairs = [(i, i + by) for i in range(size) if 0 <= i + by < size]
    return lax.ppermute(shard, axis, pairs)


def on_device(
    video, window_gaps, gn_gain, gn_bias, conv_weight, conv_bias,
    ln_gain, ln_bias, qkv_weight, out_weight, out_bias,
):
    frames, _, width, chans = video.shape
    bands = lax.axis_size("height")
    place = lax.axis_index("height")
    core = place % 2
    half = frames // 2
    cols = conv_weight.shape[1]
    swap = [(i, i ^ 1) for i in range(bands)]

    def ring(shard, by):
        return lax.ppermute(shard, "height", [(i, (i + 2 * by) % bands) for i in range(bands)])

    row = video.reshape(frames, width, chans)
    kept = lax.dynamic_slice_in_dim(row, half * core, half, axis=0)
    sent = lax.dynamic_slice_in_dim(row, half * (1 - core), half, axis=0)
    pair = jnp.stack([kept, lax.ppermute(sent, "height", swap)])
    left, right, far = ring(pair, 1), ring(pair, -1), ring(pair, 2)
    weight = lax.all_gather(conv_weight, "frames", axis=0, tiled=True)
    other = lax.ppermute(weight, "height", swap)
    by_band = conv_bias.reshape(bands, cols)
    cbias = jnp.concatenate([by_band[place], by_band[place ^ 1]])[None]
    where = jnp.stack([place // 2, core]).astype(jnp.int32)
    parts = pl.pallas_call(
        conv_kernel,
        out_shape=jax.ShapeDtypeStruct((bands, half * width, 2 * cols), BF16),
        in_specs=[SMEM] + [VMEM] * 9,
        out_specs=VMEM,
        scratch_shapes=[
            pltpu.VMEM((half, bands, width, chans), BF16),
            pltpu.VMEM((half, bands + 2, width, chans), BF16),
            pltpu.VMEM((half * bands * width + 16, 2 * cols), F32),
        ],
    )(where, pair, left, right, far, weight, other, gn_gain[None], gn_bias[None], cbias)
    parts = lax.all_to_all(parts, "height", 0, 0, tiled=True)
    cells = frames * width
    resid, norm = pl.pallas_call(
        norm_kernel,
        out_shape=[jax.ShapeDtypeStruct((cells, chans), BF16)] * 2,
        in_specs=[VMEM] * 4,
        out_specs=[VMEM] * 2,
    )(parts, row.reshape(cells, chans), ln_gain[None], ln_bias[None])
    starts = jnp.concatenate([jnp.zeros((1,), jnp.int32), jnp.cumsum(window_gaps)])
    starts = jnp.pad(starts, (0, LANES - starts.shape[0]), constant_values=-(1 << 20))
    near_ids = (lax.axis_index("frames") - 2) * frames + jnp.arange(5 * frames, dtype=jnp.int32)
    inside = (near_ids[None, :] >= starts[:, None]) & (near_ids[None, :] < starts[:, None] + WIN)
    member = inside.astype(F32)
    cover = member[:, 2 * frames : 3 * frames].T
    near = [passed(norm, "frames", by) for by in (2, 1)] + [norm]
    near += [passed(norm, "frames", by) for by in (-1, -2)]
    out = pl.pallas_call(
        attend_kernel,
        out_shape=jax.ShapeDtypeStruct((cells, chans), BF16),
        in_specs=[VMEM] * 11,
        out_specs=VMEM,
        scratch_shapes=[
            pltpu.VMEM((5, width, frames, chans), F32),
            pltpu.VMEM((5, width, frames, chans), F32),
            pltpu.VMEM((width, frames, chans), F32),
            pltpu.VMEM((width, HEADS * frames, 5 * frames), F32),
            pltpu.VMEM((width, frames, chans), F32),
        ],
    )(*near, resid, qkv_weight, out_weight, out_bias[None], member, cover)
    return out.reshape(frames, 1, width, chans)


def solution(mesh):
    placed = (
        P(("dp", "frames"), "height", None, None),
        P("dp"),
        P(),
        P(),
        P("frames", "height"),
        P(),
        P(),
        P(),
        P(),
        P(),
        P(),
    )
    return jax.shard_map(
        on_device,
        mesh=mesh,
        in_specs=placed,
        out_specs=P(("dp", "frames"), "height", None, None),
        check_vma=False,
    )
```

```python
import jax
import jax.numpy as jnp
from jax import lax
from jax.experimental import pallas as pl
from jax.experimental.pallas import tpu as pltpu
from jax.sharding import PartitionSpec as P

HEADS = 10
GROUPS = 32
WIN = 16
HEAD_DIM = 64
LANES = 128

EPSILON = 1e-05
F32 = jnp.float32
BF16 = jnp.bfloat16
VMEM = pl.BlockSpec(memory_space=pltpu.VMEM)
SMEM = pl.BlockSpec(memory_space=pltpu.SMEM)
GRANT = pltpu.CompilerParams(vmem_limit_bytes=32 << 20)
NT = (((1,), (1,)), ((), ()))


def on_chip(array):
    return pltpu.with_memory_space_constraint(array, pltpu.VMEM)


def dot(a, b):
    return jnp.dot(a, b, preferred_element_type=F32)


def exact_dot(a, b, dims=(((1,), (0,)), ((), ()))):
    return lax.dot_general(a, b, dims, precision=lax.Precision.HIGHEST, preferred_element_type=F32)


def iota(shape, dim):
    return lax.broadcasted_iota(jnp.int32, shape, dim)


def conv_kernel(
    cells_ref, weight_ref, gain_ref, bias_ref, cbias_ref, out_ref, padded, taps, shifted
):
    rows, frames, width, chans = cells_ref.shape
    chunks, outs, chunk = weight_ref.shape
    for z in range(chunks):
        taps[:, z * chunk : (z + 1) * chunk] = weight_ref[z]
    groups = (iota((chans, LANES), 0).astype(F32) + 0.5) * (GROUPS / chans)
    groups = (jnp.floor(groups) == iota((chans, LANES), 1).astype(F32)).astype(F32)
    count = rows * width * (chans // GROUPS)

    def group_mean(sums):
        per_group = exact_dot(jnp.concatenate(sums, axis=0), groups) / count
        return exact_dot(per_group, groups, NT)

    def frame(f):
        return cells_ref[:, f].reshape(rows * width, chans).astype(F32)

    mean = group_mean([jnp.sum(frame(f), axis=0, keepdims=True) for f in range(frames)])
    sums = []
    for f in range(frames):
        centred = frame(f) - mean[f : f + 1]
        sums.append(jnp.sum(centred * centred, axis=0, keepdims=True))
    inverse = lax.rsqrt(group_mean(sums) + EPSILON)
    gain, bias = gain_ref[...].reshape(1, chans), bias_ref[...].reshape(1, chans)
    edge = jnp.zeros((frames, width, chans), BF16)
    padded[0] = edge
    padded[rows + 1] = edge
    for f in range(frames):
        for r in range(rows):
            normed = cells_ref[r, f].astype(F32) - mean[f : f + 1]
            normed = normed * inverse[f : f + 1] * gain + bias
            padded[r + 1, f] = (normed / (1.0 + jnp.exp(-normed))).astype(BF16)
    flat = rows * frames * width
    column = lax.rem(iota((flat, 1), 0), width)
    total = None
    for row in range(3):
        tap = [taps[:, (3 * row + col) * chans : (3 * row + col + 1) * chans] for col in range(3)]
        term = lax.dot_general(
            padded[row : row + rows].reshape(flat, chans),
            jnp.concatenate(tap, axis=0),
            NT,
            preferred_element_type=F32,
        )
        total = term if total is None else total + term
    shifted[8 : 8 + flat] = total
    before = jnp.where(column == 0, 0.0, shifted[7 : 7 + flat, :outs])
    after = jnp.where(column == width - 1, 0.0, shifted[9 : 9 + flat, 2 * outs :])
    result = total[:, outs : 2 * outs] + before + after + cbias_ref[...]
    result = result.reshape(rows, frames * width, outs)
    for r in range(rows):
        out_ref[r] = result[r].T.astype(BF16)


def swap_matrix(frames, width, back):
    cells = frames * width
    near, far = iota((cells, cells), 1 if back else 0), iota((cells, cells), 0 if back else 1)
    same = (lax.div(near, frames) == lax.rem(far, width)) & (
        lax.rem(near, frames) == lax.div(far, width)
    )
    return same.astype(F32).astype(BF16)


def norm_kernel(part_ref, video_ref, gain_ref, bias_ref, resid_ref, norm_ref):
    frames, width, chans = video_ref.shape
    cells = frames * width
    conv_out = part_ref[...].reshape(chans, cells).astype(F32).T
    resid = (video_ref[...].reshape(cells, chans).astype(F32) + conv_out).astype(BF16)
    resid_ref[...] = resid
    floats = resid.astype(F32)
    deviation = floats - jnp.mean(floats, axis=-1, keepdims=True)
    spread = jnp.mean(deviation * deviation, axis=-1, keepdims=True)
    gain, bias = gain_ref[...].reshape(1, chans), bias_ref[...].reshape(1, chans)
    norm = (deviation * lax.rsqrt(spread + EPSILON) * gain + bias).astype(BF16)
    norm_ref[...] = dot(swap_matrix(frames, width, False), norm).astype(BF16)


def attend_kernel(
    gaps_ref, b0_ref, b1_ref, b2_ref, b3_ref, b4_ref, resid_ref, qkv_ref, out_w_ref, out_b_ref,
    out_ref, keys, values, query, scores, mixed,
):
    blocks, width, frames, chans = keys.shape
    near = blocks * frames
    stack = HEADS * frames

    def by_cell(product):
        return product.astype(BF16).astype(F32).reshape(width, frames, chans)

    query[...] = by_cell(dot(b2_ref[...], qkv_ref[:, :chans]))
    for b, ref in enumerate((b0_ref, b1_ref, b2_ref, b3_ref, b4_ref)):
        keys[b] = by_cell(dot(ref[...], qkv_ref[:, chans : 2 * chans]))
        values[b] = by_cell(dot(ref[...], qkv_ref[:, 2 * chans :]))
    window = iota((1, LANES), 1)
    start, starts = jnp.int32(0), jnp.where(window == 0, 0, -(1 << 20))
    for w in range(gaps_ref.shape[0]):
        start = start + gaps_ref[w]
        starts = jnp.where(window == w + 1, start, starts)
    ids = (lax.axis_index("frames") - 2) * frames + iota((near, LANES), 0)
    member = ((ids >= starts) & (ids < starts + WIN)).astype(F32)
    cover = member[2 * frames : 3 * frames][None]
    member = member.astype(BF16)
    head_of = lax.div(iota((HEADS, 1, chans), 2), HEAD_DIM) == iota((HEADS, 1, chans), 0)
    own = head_of.astype(F32)
    for c in range(width):
        spread = (query[c][None] * own).reshape(stack, chans).astype(BF16)
        key = keys[:, c].reshape(near, chans).astype(BF16)
        scores[c] = lax.dot_general(spread, key, NT, preferred_element_type=F32)
    flat = width * stack
    expo = jnp.exp(scores[...].reshape(flat, near) * HEAD_DIM ** (-0.5))

    def split_dot(a, dims):
        high = a.astype(BF16)
        rest = (a - high.astype(F32)).astype(BF16)
        return lax.dot_general(high, member, dims, preferred_element_type=F32) + lax.dot_general(
            rest, member, dims, preferred_element_type=F32
        )

    sums = split_dot(expo, (((1,), (0,)), ((), ()))).reshape(width * HEADS, frames, LANES)
    frame_count = jnp.sum(cover, axis=2, keepdims=True)
    coef = (cover / (frame_count * jnp.where(cover > 0, sums, 1.0))).reshape(flat, LANES)
    back = split_dot(coef, NT)
    scores[...] = (expo * back).reshape(width, stack, near)
    for c in range(width):
        value = values[:, c].reshape(near, chans).astype(BF16)
        product = dot(scores[c].astype(BF16), value).reshape(HEADS, frames, chans)
        mixed[c] = jnp.sum(jnp.where(head_of, product, 0.0), axis=0)
    joined = mixed[...].reshape(width * frames, chans).astype(BF16)
    joined = dot(swap_matrix(frames, width, True), joined).astype(BF16)
    projected = dot(joined, out_w_ref[...])
    output = resid_ref[...].astype(F32) + projected + out_b_ref[...].reshape(1, chans)
    out_ref[...] = output.astype(BF16).reshape(frames, width, chans)


def passed(shard, by):
    size = lax.axis_size("frames")
    pairs = [(i, i + by) for i in range(size) if 0 <= i + by < size]
    return lax.ppermute(shard, "frames", pairs)


def on_device(
    video, window_gaps, gn_gain, gn_bias, conv_weight, conv_bias,
    ln_gain, ln_bias, qkv_weight, out_weight, out_bias,
):
    frames, _, width, chans = video.shape
    bands = lax.axis_size("height")
    place = lax.axis_index("height")
    outs = conv_weight.shape[1]
    cells = frames * width
    row = video.reshape(frames, width, chans)
    copies = jnp.broadcast_to(row[None], (bands, frames, width, chans))
    whole = lax.all_to_all(copies, "height", 0, 0, tiled=True)
    weight = lax.all_gather(conv_weight.T, "frames", axis=0, tiled=False)
    cbias = lax.dynamic_slice_in_dim(conv_bias, place * outs, outs)[None]
    parts = pl.pallas_call(
        conv_kernel,
        out_shape=jax.ShapeDtypeStruct((bands, outs, cells), BF16),
        in_specs=[VMEM] * 5,
        out_specs=VMEM,
        compiler_params=GRANT,
        scratch_shapes=[
            pltpu.VMEM((bands + 2, frames, width, chans), BF16),
            pltpu.VMEM((outs, 9 * chans), BF16),
            pltpu.VMEM((bands * cells + 16, 3 * outs), F32),
        ],
    )(on_chip(whole), on_chip(weight), gn_gain, gn_bias, cbias)
    parts = lax.all_to_all(parts, "height", 0, 0, tiled=True)
    resid, norm = pl.pallas_call(
        norm_kernel,
        out_shape=[jax.ShapeDtypeStruct((cells, chans), BF16)] * 2,
        in_specs=[VMEM] * 4,
        out_specs=[VMEM] * 2,
        compiler_params=GRANT,
    )(on_chip(parts), row, ln_gain, ln_bias)
    near = [passed(norm, by) for by in (2, 1)] + [norm] + [passed(norm, by) for by in (-1, -2)]
    out = pl.pallas_call(
        attend_kernel,
        out_shape=jax.ShapeDtypeStruct((frames, width, chans), BF16),
        in_specs=[SMEM] + [VMEM] * 9,
        out_specs=VMEM,
        compiler_params=GRANT,
        scratch_shapes=[
            pltpu.VMEM((5, width, frames, chans), F32),
            pltpu.VMEM((5, width, frames, chans), F32),
            pltpu.VMEM((width, frames, chans), F32),
            pltpu.VMEM((width, HEADS * frames, 5 * frames), F32),
            pltpu.VMEM((width, frames, chans), F32),
        ],
    )(window_gaps, *[on_chip(n) for n in near], resid, on_chip(qkv_weight), on_chip(out_weight), out_bias)
    return out.reshape(frames, 1, width, chans)


def solution(mesh):
    placed = (
        P(("dp", "frames"), "height", None, None),
        P("dp"),
        P(),
        P(),
        P("frames", "height"),
        P(),
        P(),
        P(),
        P(),
        P(),
        P(),
    )
    return jax.shard_map(
        on_device,
        mesh=mesh,
        in_specs=placed,
        out_specs=P(("dp", "frames"), "height", None, None),
        check_vma=False,
    )
```

```python
import jax
import jax.numpy as jnp
from jax import lax
from jax.experimental import pallas as pl
from jax.experimental.pallas import tpu as pltpu
from jax.sharding import PartitionSpec as P

HEADS = 10
GROUPS = 32
WIN = 16
HEAD_DIM = 64
LANES = 128

EPSILON = 1e-05
F32 = jnp.float32
BF16 = jnp.bfloat16
VMEM = pl.BlockSpec(memory_space=pltpu.VMEM)
SMEM = pl.BlockSpec(memory_space=pltpu.SMEM)
GRANT = pltpu.CompilerParams(vmem_limit_bytes=32 << 20)
NT = (((1,), (1,)), ((), ()))


def on_chip(array):
    return pltpu.with_memory_space_constraint(array, pltpu.VMEM)


def dot(a, b):
    return jnp.dot(a, b, preferred_element_type=F32)


def exact_dot(a, b, dims=(((1,), (0,)), ((), ()))):
    return lax.dot_general(a, b, dims, precision=lax.Precision.HIGHEST, preferred_element_type=F32)


def iota(shape, dim):
    return lax.broadcasted_iota(jnp.int32, shape, dim)


def conv_kernel(
    cells_ref, weight_ref, gain_ref, bias_ref, cbias_ref, out_ref, padded, taps, shifted
):
    rows, frames, width, chans = cells_ref.shape
    chunks, outs, chunk = weight_ref.shape
    for z in range(chunks):
        taps[:, z * chunk : (z + 1) * chunk] = weight_ref[z]
    groups = (iota((chans, LANES), 0).astype(F32) + 0.5) * (GROUPS / chans)
    groups = (jnp.floor(groups) == iota((chans, LANES), 1).astype(F32)).astype(F32)
    count = rows * width * (chans // GROUPS)

    def group_mean(sums):
        per_group = exact_dot(jnp.concatenate(sums, axis=0), groups) / count
        return exact_dot(per_group, groups, NT)

    def frame(f):
        return cells_ref[:, f].reshape(rows * width, chans).astype(F32)

    mean = group_mean([jnp.sum(frame(f), axis=0, keepdims=True) for f in range(frames)])
    sums = []
    for f in range(frames):
        centred = frame(f) - mean[f : f + 1]
        sums.append(jnp.sum(centred * centred, axis=0, keepdims=True))
    inverse = lax.rsqrt(group_mean(sums) + EPSILON)
    scale, bias = inverse * gain_ref[...].reshape(1, chans), bias_ref[...].reshape(1, chans)
    edge = jnp.zeros((frames, width, chans), BF16)
    padded[0] = edge
    padded[rows + 1] = edge
    for f in range(frames):
        for r in range(rows):
            normed = cells_ref[r, f].astype(F32) - mean[f : f + 1]
            normed = 0.5 * (normed * scale[f : f + 1] + bias)
            padded[r + 1, f] = (normed + normed * jnp.tanh(normed)).astype(BF16)
    flat = rows * frames * width
    column = lax.rem(iota((flat, 1), 0), width)
    total = None
    for row in range(3):
        tap = [taps[:, (3 * row + col) * chans : (3 * row + col + 1) * chans] for col in range(3)]
        term = lax.dot_general(
            padded[row : row + rows].reshape(flat, chans),
            jnp.concatenate(tap, axis=0),
            NT,
            preferred_element_type=F32,
        )
        total = term if total is None else total + term
    shifted[8 : 8 + flat] = total
    before = jnp.where(column == 0, 0.0, shifted[7 : 7 + flat, :outs])
    after = jnp.where(column == width - 1, 0.0, shifted[9 : 9 + flat, 2 * outs :])
    result = total[:, outs : 2 * outs] + before + after + cbias_ref[...]
    result = result.reshape(rows, frames * width, outs)
    for r in range(rows):
        out_ref[r] = result[r].T.astype(BF16)


def swap_matrix(frames, width, back):
    cells = frames * width
    near, far = iota((cells, cells), 1 if back else 0), iota((cells, cells), 0 if back else 1)
    same = (lax.div(near, frames) == lax.rem(far, width)) & (
        lax.rem(near, frames) == lax.div(far, width)
    )
    return same.astype(F32).astype(BF16)


def norm_kernel(part_ref, video_ref, gain_ref, bias_ref, resid_ref, norm_ref):
    frames, width, chans = video_ref.shape
    cells = frames * width
    conv_out = part_ref[...].reshape(chans, cells).astype(F32).T
    resid = (video_ref[...].reshape(cells, chans).astype(F32) + conv_out).astype(BF16)
    resid_ref[...] = resid
    floats = resid.astype(F32)
    deviation = floats - jnp.mean(floats, axis=-1, keepdims=True)
    spread = jnp.mean(deviation * deviation, axis=-1, keepdims=True)
    gain, bias = gain_ref[...].reshape(1, chans), bias_ref[...].reshape(1, chans)
    norm = (deviation * lax.rsqrt(spread + EPSILON) * gain + bias).astype(BF16)
    norm_ref[...] = dot(swap_matrix(frames, width, False), norm).astype(BF16)


def by_cell(product, shape):
    return product.astype(BF16).astype(F32).reshape(shape)


def early_kernel(before_ref, norm_ref, after_ref, qkv_ref, query_ref, key_ref, value_ref):
    chans = norm_ref.shape[1]
    shape = query_ref.shape
    query_ref[...] = by_cell(dot(norm_ref[...], qkv_ref[:, :chans]), shape)
    for b, ref in enumerate((before_ref, norm_ref, after_ref)):
        key_ref[b] = by_cell(dot(ref[...], qkv_ref[:, chans : 2 * chans]), shape)
        value_ref[b] = by_cell(dot(ref[...], qkv_ref[:, 2 * chans :]), shape)


def attend_kernel(
    gaps_ref, b4_ref, b0_ref, query, mid_keys, mid_values, resid_ref, qkv_ref, out_w_ref,
    out_b_ref, out_ref, far_keys, far_values, scores, mixed,
):
    mids, width, frames, chans = mid_keys.shape
    near = (mids + 2) * frames
    stack = HEADS * frames
    shape = (width, frames, chans)
    for b, ref in enumerate((b0_ref, b4_ref)):
        far_keys[b] = by_cell(dot(ref[...], qkv_ref[:, chans : 2 * chans]), shape)
        far_values[b] = by_cell(dot(ref[...], qkv_ref[:, 2 * chans :]), shape)

    def at_cell(far, mid, c):
        blocks = [far[0, c]] + [mid[b, c] for b in range(mids)] + [far[1, c]]
        return jnp.concatenate(blocks, axis=0).astype(BF16)

    window = iota((1, LANES), 1)
    start, starts = jnp.int32(0), jnp.where(window == 0, 0, -(1 << 20))
    for w in range(gaps_ref.shape[0]):
        start = start + gaps_ref[w]
        starts = jnp.where(window == w + 1, start, starts)
    ids = (lax.axis_index("frames") - 2) * frames + iota((near, LANES), 0)
    member = ((ids >= starts) & (ids < starts + WIN)).astype(F32)
    cover = member[2 * frames : 3 * frames][None]
    member = member.astype(BF16)
    head_of = lax.div(iota((HEADS, 1, chans), 2), HEAD_DIM) == iota((HEADS, 1, chans), 0)
    own = head_of.astype(F32)
    for c in range(width):
        spread = (query[c][None] * own).reshape(stack, chans).astype(BF16)
        key = at_cell(far_keys, mid_keys, c)
        scores[c] = lax.dot_general(spread, key, NT, preferred_element_type=F32)
    flat = width * stack
    expo = jnp.exp(scores[...].reshape(flat, near) * HEAD_DIM ** (-0.5))

    def split_dot(a, dims):
        high = a.astype(BF16)
        rest = (a - high.astype(F32)).astype(BF16)
        return lax.dot_general(high, member, dims, preferred_element_type=F32) + lax.dot_general(
            rest, member, dims, preferred_element_type=F32
        )

    sums = split_dot(expo, (((1,), (0,)), ((), ()))).reshape(width * HEADS, frames, LANES)
    frame_count = jnp.sum(cover, axis=2, keepdims=True)
    coef = (cover / (frame_count * jnp.where(cover > 0, sums, 1.0))).reshape(flat, LANES)
    back = split_dot(coef, NT)
    scores[...] = (expo * back).reshape(width, stack, near)
    for c in range(width):
        value = at_cell(far_values, mid_values, c)
        product = dot(scores[c].astype(BF16), value).reshape(HEADS, frames, chans)
        mixed[c] = jnp.sum(jnp.where(head_of, product, 0.0), axis=0)
    joined = mixed[...].reshape(width * frames, chans).astype(BF16)
    joined = dot(swap_matrix(frames, width, True), joined).astype(BF16)
    projected = dot(joined, out_w_ref[...])
    output = resid_ref[...].astype(F32) + projected + out_b_ref[...].reshape(1, chans)
    out_ref[...] = output.astype(BF16).reshape(frames, width, chans)


def passed(shard, by):
    size = lax.axis_size("frames")
    pairs = [(i, i + by) for i in range(size) if 0 <= i + by < size]
    return lax.ppermute(shard, "frames", pairs)


def on_device(
    video, window_gaps, gn_gain, gn_bias, conv_weight, conv_bias,
    ln_gain, ln_bias, qkv_weight, out_weight, out_bias,
):
    frames, _, width, chans = video.shape
    bands = lax.axis_size("height")
    place = lax.axis_index("height")
    outs = conv_weight.shape[1]
    cells = frames * width
    row = video.reshape(frames, width, chans)
    copies = jnp.broadcast_to(row[None], (bands, frames, width, chans))
    whole = lax.all_to_all(copies, "height", 0, 0, tiled=True)
    weight = lax.all_gather(conv_weight.T, "frames", axis=0, tiled=False)
    cbias = lax.dynamic_slice_in_dim(conv_bias, place * outs, outs)[None]
    parts = pl.pallas_call(
        conv_kernel,
        out_shape=jax.ShapeDtypeStruct((bands, outs, cells), BF16),
        in_specs=[VMEM] * 5,
        out_specs=VMEM,
        compiler_params=GRANT,
        scratch_shapes=[
            pltpu.VMEM((bands + 2, frames, width, chans), BF16),
            pltpu.VMEM((outs, 9 * chans), BF16),
            pltpu.VMEM((bands * cells + 16, 3 * outs), F32),
        ],
    )(on_chip(whole), on_chip(weight), gn_gain, gn_bias, cbias)
    parts = lax.all_to_all(parts, "height", 0, 0, tiled=True)
    resid, norm = pl.pallas_call(
        norm_kernel,
        out_shape=[jax.ShapeDtypeStruct((cells, chans), BF16)] * 2,
        in_specs=[VMEM] * 4,
        out_specs=[VMEM] * 2,
        compiler_params=GRANT,
    )(on_chip(parts), row, ln_gain, ln_bias)
    b3, b1 = passed(norm, -1), passed(norm, 1)
    b4, b0 = passed(b3, -1), passed(b1, 1)
    qkv = on_chip(qkv_weight)
    own = jax.ShapeDtypeStruct((width, frames, chans), F32)
    mid = jax.ShapeDtypeStruct((3, width, frames, chans), F32)
    early = pl.pallas_call(
        early_kernel,
        out_shape=[own, mid, mid],
        in_specs=[VMEM] * 4,
        out_specs=[VMEM] * 3,
        compiler_params=GRANT,
    )(on_chip(b1), norm, on_chip(b3), qkv)
    out = pl.pallas_call(
        attend_kernel,
        out_shape=jax.ShapeDtypeStruct((frames, width, chans), BF16),
        in_specs=[SMEM] + [VMEM] * 9,
        out_specs=VMEM,
        compiler_params=GRANT,
        scratch_shapes=[
            pltpu.VMEM((2, width, frames, chans), F32),
            pltpu.VMEM((2, width, frames, chans), F32),
            pltpu.VMEM((width, HEADS * frames, 5 * frames), F32),
            pltpu.VMEM((width, frames, chans), F32),
        ],
    )(
        window_gaps, on_chip(b4), on_chip(b0), *[on_chip(n) for n in early], on_chip(resid), qkv,
        on_chip(out_weight), out_bias,
    )
    return out.reshape(frames, 1, width, chans)


def solution(mesh):
    placed = (
        P(("dp", "frames"), "height", None, None),
        P("dp"),
        P(),
        P(),
        P("frames", "height"),
        P(),
        P(),
        P(),
        P(),
        P(),
        P(),
    )
    return jax.shard_map(
        on_device,
        mesh=mesh,
        in_specs=placed,
        out_specs=P(("dp", "frames"), "height", None, None),
        check_vma=False,
    )
```

```python
import jax
import jax.numpy as jnp
from jax import lax
from jax.experimental import pallas as pl
from jax.experimental.pallas import tpu as pltpu
from jax.sharding import PartitionSpec as P

HEADS = 10
GROUPS = 32
WIN = 16
HEAD_DIM = 64
LANES = 128

EPSILON = 1e-05
F32 = jnp.float32
BF16 = jnp.bfloat16
VMEM = pl.BlockSpec(memory_space=pltpu.VMEM)
SMEM = pl.BlockSpec(memory_space=pltpu.SMEM)
GRANT = pltpu.CompilerParams(vmem_limit_bytes=32 << 20)
NT = (((1,), (1,)), ((), ()))


def on_chip(array):
    return pltpu.with_memory_space_constraint(array, pltpu.VMEM)


def dot(a, b):
    return jnp.dot(a, b, preferred_element_type=F32)


def iota(shape, dim):
    return lax.broadcasted_iota(jnp.int32, shape, dim)


def conv_kernel(
    cells_ref, weight_ref, gain_ref, bias_ref, cbias_ref, out_ref, padded, taps, shifted
):
    rows, frames, width, chans = cells_ref.shape
    chunks, outs, chunk = weight_ref.shape
    for z in range(chunks):
        taps[:, z * chunk : (z + 1) * chunk] = weight_ref[z]
    groups = (iota((chans, LANES), 0).astype(F32) + 0.5) * (GROUPS / chans)
    groups = jnp.floor(groups) == iota((chans, LANES), 1).astype(F32)
    groups = groups.astype(F32).astype(BF16)

    def pieces_dot(sums, dims):
        high = sums.astype(BF16)
        rest = sums - high.astype(F32)
        middle = rest.astype(BF16)
        low = (rest - middle.astype(F32)).astype(BF16)
        parts = jnp.concatenate([high, middle, low], axis=0)
        parts = lax.dot_general(parts, groups, dims, preferred_element_type=F32)
        count = sums.shape[0]
        return parts[:count] + parts[count : 2 * count] + parts[2 * count :]

    def group_mean(values):
        per_group = pieces_dot(values, (((1,), (0,)), ((), ()))) * (GROUPS / chans)
        return pieces_dot(per_group, NT)

    pivots, firsts, seconds = [], [], []
    for f in range(frames):
        pivot = cells_ref[0, f].astype(F32)[:1]
        first = second = jnp.zeros((width, chans), F32)
        for r in range(rows):
            away = cells_ref[r, f].astype(F32) - pivot
            first, second = first + away, second + away * away
        pivots.append(pivot)
        firsts.append(jnp.sum(first, axis=0, keepdims=True))
        seconds.append(jnp.sum(second, axis=0, keepdims=True))
    cell_count = rows * width
    first = jnp.concatenate(firsts, axis=0) / cell_count
    second = jnp.concatenate(seconds, axis=0) / cell_count
    channel_mean = jnp.concatenate(pivots, axis=0) + first
    mean = group_mean(channel_mean)
    between = channel_mean - mean
    variance = group_mean(jnp.maximum(second - first * first, 0.0) + between * between)
    inverse = lax.rsqrt(variance + EPSILON)
    scale, bias = inverse * gain_ref[...].reshape(1, chans), bias_ref[...].reshape(1, chans)
    edge = jnp.zeros((frames, width, chans), BF16)
    padded[0] = edge
    padded[rows + 1] = edge
    for f in range(frames):
        for r in range(rows):
            normed = cells_ref[r, f].astype(F32) - mean[f : f + 1]
            normed = 0.5 * (normed * scale[f : f + 1] + bias)
            padded[r + 1, f] = (normed + normed * jnp.tanh(normed)).astype(BF16)
    flat = rows * frames * width
    column = lax.rem(iota((flat, 1), 0), width)
    near = [padded[row : row + rows].reshape(flat, chans) for row in range(3)]
    tap = [taps[:, i * chans : (i + 1) * chans] for i in range(9)]
    tap = [jnp.concatenate(tap[3 * row : 3 * row + 3], axis=0) for row in range(3)]
    total = lax.dot_general(
        jnp.concatenate(near, axis=1),
        jnp.concatenate(tap, axis=1),
        NT,
        preferred_element_type=F32,
    )
    shifted[8 : 8 + flat] = total
    before = jnp.where(column == 0, 0.0, shifted[7 : 7 + flat, :outs])
    after = jnp.where(column == width - 1, 0.0, shifted[9 : 9 + flat, 2 * outs :])
    result = total[:, outs : 2 * outs] + before + after + cbias_ref[...]
    result = result.reshape(rows, frames * width, outs)
    for r in range(rows):
        out_ref[r] = result[r].T.astype(BF16)


def swap_matrix(frames, width, back):
    cells = frames * width
    near, far = iota((cells, cells), 1 if back else 0), iota((cells, cells), 0 if back else 1)
    same = (lax.div(near, frames) == lax.rem(far, width)) & (
        lax.rem(near, frames) == lax.div(far, width)
    )
    return same.astype(F32).astype(BF16)


def norm_kernel(part_ref, video_ref, gain_ref, bias_ref, resid_ref, norm_ref):
    frames, width, chans = video_ref.shape
    cells = frames * width
    conv_out = part_ref[...].reshape(chans, cells).astype(F32).T
    resid = (video_ref[...].reshape(cells, chans).astype(F32) + conv_out).astype(BF16)
    resid_ref[...] = resid
    floats = resid.astype(F32)
    deviation = floats - jnp.mean(floats, axis=-1, keepdims=True)
    spread = jnp.mean(deviation * deviation, axis=-1, keepdims=True)
    gain, bias = gain_ref[...].reshape(1, chans), bias_ref[...].reshape(1, chans)
    norm = (deviation * lax.rsqrt(spread + EPSILON) * gain + bias).astype(BF16)
    norm_ref[...] = dot(swap_matrix(frames, width, False), norm).astype(BF16)


def by_cell(product, shape):
    return product.astype(BF16).astype(F32).reshape(shape)


def early_kernel(before_ref, norm_ref, after_ref, qkv_ref, query_ref, key_ref, value_ref):
    chans = norm_ref.shape[1]
    shape = query_ref.shape
    query_ref[...] = by_cell(dot(norm_ref[...], qkv_ref[:, :chans]), shape)
    for b, ref in enumerate((before_ref, norm_ref, after_ref)):
        key_ref[b] = by_cell(dot(ref[...], qkv_ref[:, chans : 2 * chans]), shape)
        value_ref[b] = by_cell(dot(ref[...], qkv_ref[:, 2 * chans :]), shape)


def attend_kernel(
    gaps_ref, b4_ref, b0_ref, query, mid_keys, mid_values, resid_ref, qkv_ref, out_w_ref,
    out_b_ref, out_ref, far_keys, far_values, scores, mixed,
):
    mids, width, frames, chans = mid_keys.shape
    near = (mids + 2) * frames
    stack = HEADS * frames
    shape = (width, frames, chans)
    for b, ref in enumerate((b0_ref, b4_ref)):
        far_keys[b] = by_cell(dot(ref[...], qkv_ref[:, chans : 2 * chans]), shape)
        far_values[b] = by_cell(dot(ref[...], qkv_ref[:, 2 * chans :]), shape)

    def at_cell(far, mid, c):
        blocks = [far[0, c]] + [mid[b, c] for b in range(mids)] + [far[1, c]]
        return jnp.concatenate(blocks, axis=0).astype(BF16)

    window = iota((1, LANES), 1)
    start, starts = jnp.int32(0), jnp.where(window == 0, 0, -(1 << 20))
    for w in range(gaps_ref.shape[0]):
        start = start + gaps_ref[w]
        starts = jnp.where(window == w + 1, start, starts)
    ids = (lax.axis_index("frames") - 2) * frames + iota((near, LANES), 0)
    member = ((ids >= starts) & (ids < starts + WIN)).astype(F32)
    cover = member[2 * frames : 3 * frames][None]
    member = member.astype(BF16)
    head_of = lax.div(iota((HEADS, 1, chans), 2), HEAD_DIM) == iota((HEADS, 1, chans), 0)
    own = head_of.astype(F32)
    for c in range(width):
        spread = (query[c][None] * own).reshape(stack, chans).astype(BF16)
        key = at_cell(far_keys, mid_keys, c)
        scores[c] = lax.dot_general(spread, key, NT, preferred_element_type=F32)
    flat = width * stack
    expo = jnp.exp(scores[...].reshape(flat, near) * HEAD_DIM ** (-0.5))

    def split_dot(a, dims):
        high = a.astype(BF16)
        rest = (a - high.astype(F32)).astype(BF16)
        return lax.dot_general(high, member, dims, preferred_element_type=F32) + lax.dot_general(
            rest, member, dims, preferred_element_type=F32
        )

    sums = split_dot(expo, (((1,), (0,)), ((), ()))).reshape(width * HEADS, frames, LANES)
    frame_count = jnp.sum(cover, axis=2, keepdims=True)
    coef = (cover / (frame_count * jnp.where(cover > 0, sums, 1.0))).reshape(flat, LANES)
    back = split_dot(coef, NT)
    scores[...] = (expo * back).reshape(width, stack, near)
    for c in range(width):
        value = at_cell(far_values, mid_values, c)
        product = dot(scores[c].astype(BF16), value).reshape(HEADS, frames, chans)
        mixed[c] = jnp.sum(jnp.where(head_of, product, 0.0), axis=0)
    joined = mixed[...].reshape(width * frames, chans).astype(BF16)
    joined = dot(swap_matrix(frames, width, True), joined).astype(BF16)
    projected = dot(joined, out_w_ref[...])
    output = resid_ref[...].astype(F32) + projected + out_b_ref[...].reshape(1, chans)
    out_ref[...] = output.astype(BF16).reshape(frames, width, chans)


def passed(shard, by):
    size = lax.axis_size("frames")
    pairs = [(i, i + by) for i in range(size) if 0 <= i + by < size]
    return lax.ppermute(shard, "frames", pairs)


def on_device(
    video, window_gaps, gn_gain, gn_bias, conv_weight, conv_bias,
    ln_gain, ln_bias, qkv_weight, out_weight, out_bias,
):
    frames, _, width, chans = video.shape
    bands = lax.axis_size("height")
    place = lax.axis_index("height")
    outs = conv_weight.shape[1]
    cells = frames * width
    row = video.reshape(frames, width, chans)
    copies = jnp.broadcast_to(row[None], (bands, frames, width, chans))
    whole = lax.all_to_all(copies, "height", 0, 0, tiled=True)
    weight = lax.all_gather(conv_weight.T, "frames", axis=0, tiled=False)
    cbias = lax.dynamic_slice_in_dim(conv_bias, place * outs, outs)[None]
    parts = pl.pallas_call(
        conv_kernel,
        out_shape=jax.ShapeDtypeStruct((bands, outs, cells), BF16),
        in_specs=[VMEM] * 5,
        out_specs=VMEM,
        compiler_params=GRANT,
        scratch_shapes=[
            pltpu.VMEM((bands + 2, frames, width, chans), BF16),
            pltpu.VMEM((outs, 9 * chans), BF16),
            pltpu.VMEM((bands * cells + 16, 3 * outs), F32),
        ],
    )(on_chip(whole), on_chip(weight), gn_gain, gn_bias, cbias)
    parts = lax.all_to_all(parts, "height", 0, 0, tiled=True)
    resid, norm = pl.pallas_call(
        norm_kernel,
        out_shape=[jax.ShapeDtypeStruct((cells, chans), BF16)] * 2,
        in_specs=[VMEM] * 4,
        out_specs=[VMEM] * 2,
        compiler_params=GRANT,
    )(on_chip(parts), row, ln_gain, ln_bias)
    b3, b1 = passed(norm, -1), passed(norm, 1)
    b4, b0 = passed(b3, -1), passed(b1, 1)
    qkv = on_chip(qkv_weight)
    own = jax.ShapeDtypeStruct((width, frames, chans), F32)
    mid = jax.ShapeDtypeStruct((3, width, frames, chans), F32)
    early = pl.pallas_call(
        early_kernel,
        out_shape=[own, mid, mid],
        in_specs=[VMEM] * 4,
        out_specs=[VMEM] * 3,
        compiler_params=GRANT,
    )(on_chip(b1), norm, on_chip(b3), qkv)
    out = pl.pallas_call(
        attend_kernel,
        out_shape=jax.ShapeDtypeStruct((frames, width, chans), BF16),
        in_specs=[SMEM] + [VMEM] * 9,
        out_specs=VMEM,
        compiler_params=GRANT,
        scratch_shapes=[
            pltpu.VMEM((2, width, frames, chans), F32),
            pltpu.VMEM((2, width, frames, chans), F32),
            pltpu.VMEM((width, HEADS * frames, 5 * frames), F32),
            pltpu.VMEM((width, frames, chans), F32),
        ],
    )(
        window_gaps, on_chip(b4), on_chip(b0), *[on_chip(n) for n in early], on_chip(resid), qkv,
        on_chip(out_weight), out_bias,
    )
    return out.reshape(frames, 1, width, chans)


def solution(mesh):
    placed = (
        P(("dp", "frames"), "height", None, None),
        P("dp"),
        P(),
        P(),
        P("frames", "height"),
        P(),
        P(),
        P(),
        P(),
        P(),
        P(),
    )
    return jax.shard_map(
        on_device,
        mesh=mesh,
        in_specs=placed,
        out_specs=P(("dp", "frames"), "height", None, None),
        check_vma=False,
    )
```

```python
import jax
import jax.numpy as jnp
from jax import lax
from jax.experimental import pallas as pl
from jax.experimental.pallas import tpu as pltpu
from jax.sharding import PartitionSpec as P

HEADS = 10
GROUPS = 32
WIN = 16
HEAD_DIM = 64
LANES = 128

EPSILON = 1e-05
F32 = jnp.float32
BF16 = jnp.bfloat16
VMEM = pl.BlockSpec(memory_space=pltpu.VMEM)
SMEM = pl.BlockSpec(memory_space=pltpu.SMEM)
GRANT = pltpu.CompilerParams(vmem_limit_bytes=32 << 20)
NT = (((1,), (1,)), ((), ()))


def on_chip(array):
    return pltpu.with_memory_space_constraint(array, pltpu.VMEM)


def dot(a, b):
    return jnp.dot(a, b, preferred_element_type=F32)


def iota(shape, dim):
    return lax.broadcasted_iota(jnp.int32, shape, dim)


def conv_kernel(
    cells_ref, weight_ref, gain_ref, bias_ref, cbias_ref, out_ref, padded, taps
):
    rows, frames, width, chans = cells_ref.shape
    chunks, outs, chunk = weight_ref.shape
    for z in range(chunks):
        taps[:, z * chunk : (z + 1) * chunk] = weight_ref[z]
    groups = (iota((chans, LANES), 0).astype(F32) + 0.5) * (GROUPS / chans)
    groups = jnp.floor(groups) == iota((chans, LANES), 1).astype(F32)
    groups = groups.astype(F32).astype(BF16)

    def pieces_dot(sums, dims):
        high = sums.astype(BF16)
        rest = sums - high.astype(F32)
        middle = rest.astype(BF16)
        low = (rest - middle.astype(F32)).astype(BF16)
        parts = jnp.concatenate([high, middle, low], axis=0)
        parts = lax.dot_general(parts, groups, dims, preferred_element_type=F32)
        count = sums.shape[0]
        return parts[:count] + parts[count : 2 * count] + parts[2 * count :]

    def group_mean(values):
        per_group = pieces_dot(values, (((1,), (0,)), ((), ()))) * (GROUPS / chans)
        return pieces_dot(per_group, NT)

    pivots, firsts, seconds = [], [], []
    for f in range(frames):
        pivot = cells_ref[0, f].astype(F32)[:1]
        first = second = jnp.zeros((width, chans), F32)
        for r in range(rows):
            away = cells_ref[r, f].astype(F32) - pivot
            first, second = first + away, second + away * away
        pivots.append(pivot)
        firsts.append(jnp.sum(first, axis=0, keepdims=True))
        seconds.append(jnp.sum(second, axis=0, keepdims=True))
    cell_count = rows * width
    first = jnp.concatenate(firsts, axis=0) / cell_count
    second = jnp.concatenate(seconds, axis=0) / cell_count
    channel_mean = jnp.concatenate(pivots, axis=0) + first
    mean = group_mean(channel_mean)
    between = channel_mean - mean
    variance = group_mean(jnp.maximum(second - first * first, 0.0) + between * between)
    inverse = lax.rsqrt(variance + EPSILON)
    scale, bias = inverse * gain_ref[...].reshape(1, chans), bias_ref[...].reshape(1, chans)
    edge = jnp.zeros((frames, width, chans), BF16)
    padded[0] = edge
    padded[rows + 1] = edge
    for f in range(frames):
        for r in range(rows):
            normed = cells_ref[r, f].astype(F32) - mean[f : f + 1]
            normed = 0.5 * (normed * scale[f : f + 1] + bias)
            padded[r + 1, f] = (normed + normed * jnp.tanh(normed)).astype(BF16)
    flat = rows * frames * width
    near = [padded[row : row + rows].reshape(flat, chans) for row in range(3)]
    tap = [taps[:, i * chans : (i + 1) * chans] for i in range(9)]
    tap = [jnp.concatenate(tap[3 * row : 3 * row + 3], axis=0) for row in range(3)]
    total = lax.dot_general(
        jnp.concatenate(tap, axis=1),
        jnp.concatenate(near, axis=1),
        NT,
        preferred_element_type=F32,
    )
    lanes = frames * width
    column = lax.rem(iota((1, lanes), 1), width)
    for r in range(rows):
        left, middle, right = [
            total[col * outs : (col + 1) * outs, r * lanes : (r + 1) * lanes] for col in range(3)
        ]
        left = jnp.where(column == 0, 0.0, pltpu.roll(left, 1, 1))
        right = jnp.where(column == width - 1, 0.0, pltpu.roll(right, lanes - 1, 1))
        out_ref[r] = (middle + left + right + cbias_ref[...]).astype(BF16)


def swap_matrix(frames, width, back):
    cells = frames * width
    near, far = iota((cells, cells), 1 if back else 0), iota((cells, cells), 0 if back else 1)
    same = (lax.div(near, frames) == lax.rem(far, width)) & (
        lax.rem(near, frames) == lax.div(far, width)
    )
    return same.astype(F32).astype(BF16)


def norm_kernel(part_ref, video_ref, gain_ref, bias_ref, resid_ref, norm_ref):
    frames, width, chans = video_ref.shape
    cells = frames * width
    conv_out = part_ref[...].reshape(chans, cells).astype(F32).T
    resid = (video_ref[...].reshape(cells, chans).astype(F32) + conv_out).astype(BF16)
    resid_ref[...] = resid
    floats = resid.astype(F32)
    deviation = floats - jnp.mean(floats, axis=-1, keepdims=True)
    spread = jnp.mean(deviation * deviation, axis=-1, keepdims=True)
    gain, bias = gain_ref[...].reshape(1, chans), bias_ref[...].reshape(1, chans)
    norm = (deviation * lax.rsqrt(spread + EPSILON) * gain + bias).astype(BF16)
    norm_ref[...] = dot(swap_matrix(frames, width, False), norm).astype(BF16)


def by_cell(product, shape):
    return product.astype(BF16).astype(F32).reshape(shape)


def early_kernel(before_ref, norm_ref, after_ref, qkv_ref, query_ref, key_ref, value_ref):
    chans = norm_ref.shape[1]
    shape = query_ref.shape
    query_ref[...] = by_cell(dot(norm_ref[...], qkv_ref[:, :chans]), shape)
    for b, ref in enumerate((before_ref, norm_ref, after_ref)):
        key_ref[b] = by_cell(dot(ref[...], qkv_ref[:, chans : 2 * chans]), shape)
        value_ref[b] = by_cell(dot(ref[...], qkv_ref[:, 2 * chans :]), shape)


def attend_kernel(
    gaps_ref, b4_ref, b0_ref, query, mid_keys, mid_values, resid_ref, qkv_ref, out_w_ref,
    out_b_ref, out_ref, far_keys, far_values, scores, mixed,
):
    mids, width, frames, chans = mid_keys.shape
    near = (mids + 2) * frames
    stack = HEADS * frames
    shape = (width, frames, chans)
    for b, ref in enumerate((b0_ref, b4_ref)):
        far_keys[b] = by_cell(dot(ref[...], qkv_ref[:, chans : 2 * chans]), shape)
        far_values[b] = by_cell(dot(ref[...], qkv_ref[:, 2 * chans :]), shape)

    def at_cell(far, mid, c):
        blocks = [far[0, c]] + [mid[b, c] for b in range(mids)] + [far[1, c]]
        return jnp.concatenate(blocks, axis=0).astype(BF16)

    window = iota((1, LANES), 1)
    start, starts = jnp.int32(0), jnp.where(window == 0, 0, -(1 << 20))
    for w in range(gaps_ref.shape[0]):
        start = start + gaps_ref[w]
        starts = jnp.where(window == w + 1, start, starts)
    ids = (lax.axis_index("frames") - 2) * frames + iota((near, LANES), 0)
    member = ((ids >= starts) & (ids < starts + WIN)).astype(F32)
    cover = member[2 * frames : 3 * frames][None]
    member = member.astype(BF16)
    head_of = lax.div(iota((HEADS, 1, chans), 2), HEAD_DIM) == iota((HEADS, 1, chans), 0)
    own = head_of.astype(F32)
    for c in range(width):
        spread = (query[c][None] * own).reshape(stack, chans).astype(BF16)
        key = at_cell(far_keys, mid_keys, c)
        scores[c] = lax.dot_general(spread, key, NT, preferred_element_type=F32)
    flat = width * stack
    expo = jnp.exp(scores[...].reshape(flat, near) * HEAD_DIM ** (-0.5))

    def split_dot(a, dims):
        high = a.astype(BF16)
        rest = (a - high.astype(F32)).astype(BF16)
        return lax.dot_general(high, member, dims, preferred_element_type=F32) + lax.dot_general(
            rest, member, dims, preferred_element_type=F32
        )

    sums = split_dot(expo, (((1,), (0,)), ((), ()))).reshape(width * HEADS, frames, LANES)
    frame_count = jnp.sum(cover, axis=2, keepdims=True)
    coef = (cover / (frame_count * jnp.where(cover > 0, sums, 1.0))).reshape(flat, LANES)
    back = split_dot(coef, NT)
    scores[...] = (expo * back).reshape(width, stack, near)
    for c in range(width):
        value = at_cell(far_values, mid_values, c)
        product = dot(scores[c].astype(BF16), value).reshape(HEADS, frames, chans)
        mixed[c] = jnp.sum(jnp.where(head_of, product, 0.0), axis=0)
    joined = mixed[...].reshape(width * frames, chans).astype(BF16)
    joined = dot(swap_matrix(frames, width, True), joined).astype(BF16)
    projected = dot(joined, out_w_ref[...])
    output = resid_ref[...].astype(F32) + projected + out_b_ref[...].reshape(1, chans)
    out_ref[...] = output.astype(BF16).reshape(frames, width, chans)


def passed(shard, by):
    size = lax.axis_size("frames")
    pairs = [(i, i + by) for i in range(size) if 0 <= i + by < size]
    return lax.ppermute(shard, "frames", pairs)


def on_device(
    video, window_gaps, gn_gain, gn_bias, conv_weight, conv_bias,
    ln_gain, ln_bias, qkv_weight, out_weight, out_bias,
):
    frames, _, width, chans = video.shape
    bands = lax.axis_size("height")
    place = lax.axis_index("height")
    outs = conv_weight.shape[1]
    cells = frames * width
    row = video.reshape(frames, width, chans)
    copies = jnp.broadcast_to(row[None], (bands, frames, width, chans))
    whole = lax.all_to_all(copies, "height", 0, 0, tiled=True)
    weight = lax.all_gather(conv_weight.T, "frames", axis=0, tiled=False)
    cbias = lax.dynamic_slice_in_dim(conv_bias, place * outs, outs)[:, None]
    parts = pl.pallas_call(
        conv_kernel,
        out_shape=jax.ShapeDtypeStruct((bands, outs, cells), BF16),
        in_specs=[VMEM] * 5,
        out_specs=VMEM,
        compiler_params=GRANT,
        scratch_shapes=[
            pltpu.VMEM((bands + 2, frames, width, chans), BF16),
            pltpu.VMEM((outs, 9 * chans), BF16),
        ],
    )(on_chip(whole), on_chip(weight), gn_gain, gn_bias, cbias)
    parts = lax.all_to_all(parts, "height", 0, 0, tiled=True)
    resid, norm = pl.pallas_call(
        norm_kernel,
        out_shape=[jax.ShapeDtypeStruct((cells, chans), BF16)] * 2,
        in_specs=[VMEM] * 4,
        out_specs=[VMEM] * 2,
        compiler_params=GRANT,
    )(on_chip(parts), row, ln_gain, ln_bias)
    b3, b1 = passed(norm, -1), passed(norm, 1)
    b4, b0 = passed(b3, -1), passed(b1, 1)
    qkv = on_chip(qkv_weight)
    own = jax.ShapeDtypeStruct((width, frames, chans), F32)
    mid = jax.ShapeDtypeStruct((3, width, frames, chans), F32)
    early = pl.pallas_call(
        early_kernel,
        out_shape=[own, mid, mid],
        in_specs=[VMEM] * 4,
        out_specs=[VMEM] * 3,
        compiler_params=GRANT,
    )(on_chip(b1), norm, on_chip(b3), qkv)
    out = pl.pallas_call(
        attend_kernel,
        out_shape=jax.ShapeDtypeStruct((frames, width, chans), BF16),
        in_specs=[SMEM] + [VMEM] * 9,
        out_specs=VMEM,
        compiler_params=GRANT,
        scratch_shapes=[
            pltpu.VMEM((2, width, frames, chans), F32),
            pltpu.VMEM((2, width, frames, chans), F32),
            pltpu.VMEM((width, HEADS * frames, 5 * frames), F32),
            pltpu.VMEM((width, frames, chans), F32),
        ],
    )(
        window_gaps, on_chip(b4), on_chip(b0), *[on_chip(n) for n in early], on_chip(resid), qkv,
        on_chip(out_weight), out_bias,
    )
    return out.reshape(frames, 1, width, chans)


def solution(mesh):
    placed = (
        P(("dp", "frames"), "height", None, None),
        P("dp"),
        P(),
        P(),
        P("frames", "height"),
        P(),
        P(),
        P(),
        P(),
        P(),
        P(),
    )
    return jax.shard_map(
        on_device,
        mesh=mesh,
        in_specs=placed,
        out_specs=P(("dp", "frames"), "height", None, None),
        check_vma=False,
    )
```

```python
import jax
import jax.numpy as jnp
from jax import lax
from jax.experimental import pallas as pl
from jax.experimental.pallas import tpu as pltpu
from jax.sharding import PartitionSpec as P

HEADS = 10
GROUPS = 32
WIN = 16
HEAD_DIM = 64
LANES = 128

EPSILON = 1e-05
F32 = jnp.float32
BF16 = jnp.bfloat16
VMEM = pl.BlockSpec(memory_space=pltpu.VMEM)
SMEM = pl.BlockSpec(memory_space=pltpu.SMEM)
GRANT = pltpu.CompilerParams(vmem_limit_bytes=32 << 20)
NT = (((1,), (1,)), ((), ()))


def on_chip(array):
    return pltpu.with_memory_space_constraint(array, pltpu.VMEM)


def dot(a, b):
    return jnp.dot(a, b, preferred_element_type=F32)


def iota(shape, dim):
    return lax.broadcasted_iota(jnp.int32, shape, dim)


def conv_kernel(
    cells_ref, weight_ref, gain_ref, bias_ref, cbias_ref, out_ref, padded, taps
):
    rows, frames, width, chans = cells_ref.shape
    chunks, outs, chunk = weight_ref.shape
    for z in range(chunks):
        taps[:, z * chunk : (z + 1) * chunk] = weight_ref[z]
    groups = (iota((chans, LANES), 0).astype(F32) + 0.5) * (GROUPS / chans)
    groups = jnp.floor(groups) == iota((chans, LANES), 1).astype(F32)
    groups = groups.astype(F32).astype(BF16)

    def pieces_dot(sums, dims):
        high = sums.astype(BF16)
        rest = sums - high.astype(F32)
        middle = rest.astype(BF16)
        low = (rest - middle.astype(F32)).astype(BF16)
        parts = jnp.concatenate([high, middle, low], axis=0)
        parts = lax.dot_general(parts, groups, dims, preferred_element_type=F32)
        count = sums.shape[0]
        return parts[:count] + parts[count : 2 * count] + parts[2 * count :]

    def group_mean(values):
        per_group = pieces_dot(values, (((1,), (0,)), ((), ()))) * (GROUPS / chans)
        return pieces_dot(per_group, NT)

    pivots, firsts, seconds = [], [], []
    for f in range(frames):
        pivot = cells_ref[0, f].astype(F32)[:1]
        first = second = jnp.zeros((width, chans), F32)
        for r in range(rows):
            away = cells_ref[r, f].astype(F32) - pivot
            first, second = first + away, second + away * away
        pivots.append(pivot)
        firsts.append(jnp.sum(first, axis=0, keepdims=True))
        seconds.append(jnp.sum(second, axis=0, keepdims=True))
    cell_count = rows * width
    first = jnp.concatenate(firsts, axis=0) / cell_count
    second = jnp.concatenate(seconds, axis=0) / cell_count
    channel_mean = jnp.concatenate(pivots, axis=0) + first
    mean = group_mean(channel_mean)
    between = channel_mean - mean
    variance = group_mean(jnp.maximum(second - first * first, 0.0) + between * between)
    inverse = lax.rsqrt(variance + EPSILON)
    scale, bias = inverse * gain_ref[...].reshape(1, chans), bias_ref[...].reshape(1, chans)
    edge = jnp.zeros((frames, width, chans), BF16)
    padded[0] = edge
    padded[rows + 1] = edge
    for f in range(frames):
        for r in range(rows):
            normed = cells_ref[r, f].astype(F32) - mean[f : f + 1]
            normed = 0.5 * (normed * scale[f : f + 1] + bias)
            padded[r + 1, f] = (normed + normed * jnp.tanh(normed)).astype(BF16)
    flat = rows * frames * width
    near = [padded[row : row + rows].reshape(flat, chans) for row in range(3)]
    tap = [taps[:, i * chans : (i + 1) * chans] for i in range(9)]
    tap = [jnp.concatenate(tap[3 * row : 3 * row + 3], axis=0) for row in range(3)]
    total = lax.dot_general(
        jnp.concatenate(tap, axis=1),
        jnp.concatenate(near, axis=1),
        NT,
        preferred_element_type=F32,
    )
    lanes = frames * width
    column = lax.rem(iota((1, lanes), 1), width)
    for r in range(rows):
        left, middle, right = [
            total[col * outs : (col + 1) * outs, r * lanes : (r + 1) * lanes] for col in range(3)
        ]
        left = jnp.where(column == 0, 0.0, pltpu.roll(left, 1, 1))
        right = jnp.where(column == width - 1, 0.0, pltpu.roll(right, lanes - 1, 1))
        out_ref[r] = (middle + left + right + cbias_ref[...]).astype(BF16)


def swap_matrix(frames, width, back):
    cells = frames * width
    near, far = iota((cells, cells), 1 if back else 0), iota((cells, cells), 0 if back else 1)
    same = (lax.div(near, frames) == lax.rem(far, width)) & (
        lax.rem(near, frames) == lax.div(far, width)
    )
    return same.astype(F32).astype(BF16)


def norm_kernel(part_ref, video_ref, gain_ref, bias_ref, resid_ref, norm_ref):
    frames, width, chans = video_ref.shape
    cells = frames * width
    conv_out = part_ref[...].reshape(chans, cells).astype(F32).T
    resid = (video_ref[...].reshape(cells, chans).astype(F32) + conv_out).astype(BF16)
    resid_ref[...] = resid
    floats = resid.astype(F32)
    deviation = floats - jnp.mean(floats, axis=-1, keepdims=True)
    spread = jnp.mean(deviation * deviation, axis=-1, keepdims=True)
    gain, bias = gain_ref[...].reshape(1, chans), bias_ref[...].reshape(1, chans)
    norm = (deviation * lax.rsqrt(spread + EPSILON) * gain + bias).astype(BF16)
    norm_ref[...] = dot(swap_matrix(frames, width, False), norm).astype(BF16)


def by_cell(product, shape):
    return product.astype(BF16).astype(F32).reshape(shape)


def early_kernel(
    gaps_ref, before_ref, norm_ref, after_ref, qkv_ref, member_ref, query_ref, key_ref, value_ref
):
    chans = norm_ref.shape[1]
    query_ref[...] = by_cell(dot(norm_ref[...], qkv_ref[:, :chans]), query_ref.shape)
    rows = jnp.concatenate([before_ref[...], norm_ref[...], after_ref[...]], axis=0)
    key_ref[...] = by_cell(dot(rows, qkv_ref[:, chans : 2 * chans]), key_ref.shape)
    value_ref[...] = by_cell(dot(rows, qkv_ref[:, 2 * chans :]), value_ref.shape)
    frames = query_ref.shape[1]
    window = iota((1, LANES), 1)
    start, starts = jnp.int32(0), jnp.where(window == 0, 0, -(1 << 20))
    for w in range(gaps_ref.shape[0]):
        start = start + gaps_ref[w]
        starts = jnp.where(window == w + 1, start, starts)
    ids = (lax.axis_index("frames") - 2) * frames + iota(member_ref.shape, 0)
    member_ref[...] = ((ids >= starts) & (ids < starts + WIN)).astype(F32)


def attend_kernel(
    b4_ref, b0_ref, member_ref, query, mid_keys, mid_values, resid_ref, qkv_ref, out_w_ref,
    out_b_ref, out_ref, far_keys, far_values, scores, mixed,
):
    mids, width, frames, chans = mid_keys.shape
    near = (mids + 2) * frames
    stack = HEADS * frames
    rows = jnp.concatenate([b0_ref[...], b4_ref[...]], axis=0)
    far_keys[...] = by_cell(dot(rows, qkv_ref[:, chans : 2 * chans]), far_keys.shape)
    far_values[...] = by_cell(dot(rows, qkv_ref[:, 2 * chans :]), far_values.shape)

    def at_cell(far, mid, c):
        blocks = [far[0, c]] + [mid[b, c] for b in range(mids)] + [far[1, c]]
        return jnp.concatenate(blocks, axis=0).astype(BF16)

    member = member_ref[...]
    cover = member[2 * frames : 3 * frames][None]
    member = member.astype(BF16)
    head_of = lax.div(iota((HEADS, 1, chans), 2), HEAD_DIM) == iota((HEADS, 1, chans), 0)
    own = head_of.astype(F32)
    for c in range(width):
        spread = (query[c][None] * own).reshape(stack, chans).astype(BF16)
        key = at_cell(far_keys, mid_keys, c)
        scores[c] = lax.dot_general(spread, key, NT, preferred_element_type=F32)
    flat = width * stack
    expo = jnp.exp(scores[...].reshape(flat, near) * HEAD_DIM ** (-0.5))

    def split_dot(a, dims):
        high = jnp.minimum(a, float(jnp.finfo(BF16).max)).astype(BF16)
        rest = (a - high.astype(F32)).astype(BF16)
        return lax.dot_general(high, member, dims, preferred_element_type=F32) + lax.dot_general(
            rest, member, dims, preferred_element_type=F32
        )

    sums = split_dot(expo, (((1,), (0,)), ((), ()))).reshape(width * HEADS, frames, LANES)
    frame_count = jnp.sum(cover, axis=2, keepdims=True)
    coef = (cover / (frame_count * jnp.where(cover > 0, sums, 1.0))).reshape(flat, LANES)
    back = split_dot(coef, NT)
    scores[...] = (expo * back).reshape(width, stack, near)
    for c in range(width):
        value = at_cell(far_values, mid_values, c)
        product = dot(scores[c].astype(BF16), value).reshape(HEADS, frames, chans)
        mixed[c] = jnp.sum(jnp.where(head_of, product, 0.0), axis=0)
    joined = mixed[...].reshape(width * frames, chans).astype(BF16)
    joined = dot(swap_matrix(frames, width, True), joined).astype(BF16)
    projected = dot(joined, out_w_ref[...])
    output = resid_ref[...].astype(F32) + projected + out_b_ref[...].reshape(1, chans)
    out_ref[...] = output.astype(BF16).reshape(frames, width, chans)


def passed(shard, by):
    size = lax.axis_size("frames")
    pairs = [(i, i + by) for i in range(size) if 0 <= i + by < size]
    return lax.ppermute(shard, "frames", pairs)


def on_device(
    video, window_gaps, gn_gain, gn_bias, conv_weight, conv_bias,
    ln_gain, ln_bias, qkv_weight, out_weight, out_bias,
):
    frames, _, width, chans = video.shape
    bands = lax.axis_size("height")
    place = lax.axis_index("height")
    outs = conv_weight.shape[1]
    cells = frames * width
    row = video.reshape(frames, width, chans)
    copies = jnp.broadcast_to(row[None], (bands, frames, width, chans))
    whole = lax.all_to_all(copies, "height", 0, 0, tiled=True)
    weight = lax.all_gather(conv_weight.T, "frames", axis=0, tiled=False)
    cbias = lax.dynamic_slice_in_dim(conv_bias, place * outs, outs)[:, None]
    parts = pl.pallas_call(
        conv_kernel,
        out_shape=jax.ShapeDtypeStruct((bands, outs, cells), BF16),
        in_specs=[VMEM] * 5,
        out_specs=VMEM,
        compiler_params=GRANT,
        scratch_shapes=[
            pltpu.VMEM((bands + 2, frames, width, chans), BF16),
            pltpu.VMEM((outs, 9 * chans), BF16),
        ],
    )(on_chip(whole), on_chip(weight), gn_gain, gn_bias, cbias)
    parts = lax.all_to_all(parts, "height", 0, 0, tiled=True)
    resid, norm = pl.pallas_call(
        norm_kernel,
        out_shape=[jax.ShapeDtypeStruct((cells, chans), BF16)] * 2,
        in_specs=[VMEM] * 4,
        out_specs=[VMEM] * 2,
        compiler_params=GRANT,
    )(on_chip(parts), row, ln_gain, ln_bias)
    b3, b1 = passed(norm, -1), passed(norm, 1)
    b4, b0 = passed(b3, -1), passed(b1, 1)
    qkv = on_chip(qkv_weight)
    own = jax.ShapeDtypeStruct((width, frames, chans), F32)
    mid = jax.ShapeDtypeStruct((3, width, frames, chans), F32)
    early = pl.pallas_call(
        early_kernel,
        out_shape=[jax.ShapeDtypeStruct((5 * frames, LANES), F32), own, mid, mid],
        in_specs=[SMEM] + [VMEM] * 4,
        out_specs=[VMEM] * 4,
        compiler_params=GRANT,
    )(window_gaps, on_chip(b1), norm, on_chip(b3), qkv)
    out = pl.pallas_call(
        attend_kernel,
        out_shape=jax.ShapeDtypeStruct((frames, width, chans), BF16),
        in_specs=[VMEM] * 10,
        out_specs=VMEM,
        compiler_params=GRANT,
        scratch_shapes=[
            pltpu.VMEM((2, width, frames, chans), F32),
            pltpu.VMEM((2, width, frames, chans), F32),
            pltpu.VMEM((width, HEADS * frames, 5 * frames), F32),
            pltpu.VMEM((width, frames, chans), F32),
        ],
    )(
        on_chip(b4), on_chip(b0), *[on_chip(n) for n in early], on_chip(resid), qkv,
        on_chip(out_weight), on_chip(out_bias),
    )
    return out.reshape(frames, 1, width, chans)


def solution(mesh):
    placed = (
        P(("dp", "frames"), "height", None, None),
        P("dp"),
        P(),
        P(),
        P("frames", "height"),
        P(),
        P(),
        P(),
        P(),
        P(),
        P(),
    )
    return jax.shard_map(
        on_device,
        mesh=mesh,
        in_specs=placed,
        out_specs=P(("dp", "frames"), "height", None, None),
        check_vma=False,
    )
```

```python
import jax
import jax.numpy as jnp
from jax import lax
from jax.experimental import pallas as pl
from jax.experimental.pallas import tpu as pltpu
from jax.sharding import PartitionSpec as P

HEADS = 10
GROUPS = 32
WIN = 16
HEAD_DIM = 64
LANES = 128

EPSILON = 1e-05
F32 = jnp.float32
BF16 = jnp.bfloat16
VMEM = pl.BlockSpec(memory_space=pltpu.VMEM)
SMEM = pl.BlockSpec(memory_space=pltpu.SMEM)
GRANT = pltpu.CompilerParams(vmem_limit_bytes=32 << 20)
NT = (((1,), (1,)), ((), ()))


def on_chip(array):
    return pltpu.with_memory_space_constraint(array, pltpu.VMEM)


def dot(a, b):
    return jnp.dot(a, b, preferred_element_type=F32)


def iota(shape, dim):
    return lax.broadcasted_iota(jnp.int32, shape, dim)


def conv_kernel(
    cells_ref, weight_ref, gain_ref, bias_ref, cbias_ref, out_ref, padded, taps
):
    rows, frames, width, chans = cells_ref.shape
    chunks, outs, chunk = weight_ref.shape
    for z in range(chunks):
        taps[:, z * chunk : (z + 1) * chunk] = weight_ref[z]
    groups = (iota((chans, LANES), 0).astype(F32) + 0.5) * (GROUPS / chans)
    groups = jnp.floor(groups) == iota((chans, LANES), 1).astype(F32)
    groups = groups.astype(F32).astype(BF16)

    def pieces_dot(sums, dims):
        high = sums.astype(BF16)
        rest = sums - high.astype(F32)
        middle = rest.astype(BF16)
        low = (rest - middle.astype(F32)).astype(BF16)
        parts = jnp.concatenate([high, middle, low], axis=0)
        parts = lax.dot_general(parts, groups, dims, preferred_element_type=F32)
        count = sums.shape[0]
        return parts[:count] + parts[count : 2 * count] + parts[2 * count :]

    def group_mean(values):
        per_group = pieces_dot(values, (((1,), (0,)), ((), ()))) * (GROUPS / chans)
        return pieces_dot(per_group, NT)

    pivots, firsts, seconds = [], [], []
    for f in range(frames):
        pivot = cells_ref[0, f].astype(F32)[:1]
        first = second = jnp.zeros((width, chans), F32)
        for r in range(rows):
            away = cells_ref[r, f].astype(F32) - pivot
            first, second = first + away, second + away * away
        pivots.append(pivot)
        firsts.append(jnp.sum(first, axis=0, keepdims=True))
        seconds.append(jnp.sum(second, axis=0, keepdims=True))
    cell_count = rows * width
    first = jnp.concatenate(firsts, axis=0) / cell_count
    second = jnp.concatenate(seconds, axis=0) / cell_count
    channel_mean = jnp.concatenate(pivots, axis=0) + first
    mean = group_mean(channel_mean)
    between = channel_mean - mean
    variance = group_mean(jnp.maximum(second - first * first, 0.0) + between * between)
    inverse = lax.rsqrt(variance + EPSILON)
    scale, bias = inverse * gain_ref[...].reshape(1, chans), bias_ref[...].reshape(1, chans)
    edge = jnp.zeros((frames, width, chans), BF16)
    padded[0] = edge
    padded[rows + 1] = edge
    for f in range(frames):
        for r in range(rows):
            normed = cells_ref[r, f].astype(F32) - mean[f : f + 1]
            normed = 0.5 * (normed * scale[f : f + 1] + bias)
            padded[r + 1, f] = (normed + normed * jnp.tanh(normed)).astype(BF16)
    flat = rows * frames * width
    near = [padded[row : row + rows].reshape(flat, chans) for row in range(3)]
    tap = [taps[:, i * chans : (i + 1) * chans] for i in range(9)]
    tap = [jnp.concatenate(tap[3 * row : 3 * row + 3], axis=0) for row in range(3)]
    total = lax.dot_general(
        jnp.concatenate(tap, axis=1),
        jnp.concatenate(near, axis=1),
        NT,
        preferred_element_type=F32,
    )
    lanes = frames * width
    cbias = jnp.broadcast_to(cbias_ref[...], (8, outs)).T[:, :1]
    column = lax.rem(iota((1, lanes), 1), width)
    for r in range(rows):
        left, middle, right = [
            total[col * outs : (col + 1) * outs, r * lanes : (r + 1) * lanes] for col in range(3)
        ]
        left = jnp.where(column == 0, 0.0, pltpu.roll(left, 1, 1))
        right = jnp.where(column == width - 1, 0.0, pltpu.roll(right, lanes - 1, 1))
        out_ref[r] = (middle + left + right + cbias).astype(BF16)


def swap_matrix(frames, width, back):
    cells = frames * width
    near, far = iota((cells, cells), 1 if back else 0), iota((cells, cells), 0 if back else 1)
    same = (lax.div(near, frames) == lax.rem(far, width)) & (
        lax.rem(near, frames) == lax.div(far, width)
    )
    return same.astype(F32).astype(BF16)


def norm_kernel(part_ref, video_ref, gain_ref, bias_ref, resid_ref, norm_ref):
    frames, width, chans = video_ref.shape
    cells = frames * width
    conv_out = part_ref[...].reshape(chans, cells).astype(F32).T
    resid = (video_ref[...].reshape(cells, chans).astype(F32) + conv_out).astype(BF16)
    resid_ref[...] = resid
    floats = resid.astype(F32)
    deviation = floats - jnp.mean(floats, axis=-1, keepdims=True)
    spread = jnp.mean(deviation * deviation, axis=-1, keepdims=True)
    gain, bias = gain_ref[...].reshape(1, chans), bias_ref[...].reshape(1, chans)
    norm = (deviation * lax.rsqrt(spread + EPSILON) * gain + bias).astype(BF16)
    norm_ref[...] = dot(swap_matrix(frames, width, False), norm).astype(BF16)


def by_cell(product, shape):
    return product.astype(BF16).astype(F32).reshape(shape)


def early_kernel(
    gaps_ref, before_ref, norm_ref, after_ref, qkv_ref, member_ref, query_ref, key_ref, value_ref
):
    chans = norm_ref.shape[1]
    query_ref[...] = by_cell(dot(norm_ref[...], qkv_ref[:, :chans]), query_ref.shape)
    rows = jnp.concatenate([before_ref[...], norm_ref[...], after_ref[...]], axis=0)
    key_ref[...] = by_cell(dot(rows, qkv_ref[:, chans : 2 * chans]), key_ref.shape)
    value_ref[...] = by_cell(dot(rows, qkv_ref[:, 2 * chans :]), value_ref.shape)
    frames = query_ref.shape[1]
    window = iota((1, LANES), 1)
    start, starts = jnp.int32(0), jnp.where(window == 0, 0, -(1 << 20))
    for w in range(gaps_ref.shape[0]):
        start = start + gaps_ref[w]
        starts = jnp.where(window == w + 1, start, starts)
    ids = (lax.axis_index("frames") - 2) * frames + iota(member_ref.shape, 0)
    member_ref[...] = ((ids >= starts) & (ids < starts + WIN)).astype(F32)


def attend_kernel(
    b4_ref, b0_ref, member_ref, query, mid_keys, mid_values, resid_ref, qkv_ref, out_w_ref,
    out_b_ref, out_ref, far_keys, far_values, scores, mixed,
):
    mids, width, frames, chans = mid_keys.shape
    near = (mids + 2) * frames
    stack = HEADS * frames
    rows = jnp.concatenate([b0_ref[...], b4_ref[...]], axis=0)
    far_keys[...] = by_cell(dot(rows, qkv_ref[:, chans : 2 * chans]), far_keys.shape)
    far_values[...] = by_cell(dot(rows, qkv_ref[:, 2 * chans :]), far_values.shape)

    def at_cell(far, mid, c):
        blocks = [far[0, c]] + [mid[b, c] for b in range(mids)] + [far[1, c]]
        return jnp.concatenate(blocks, axis=0).astype(BF16)

    member = member_ref[...]
    cover = member[2 * frames : 3 * frames][None]
    member = member.astype(BF16)
    head_of = lax.div(iota((HEADS, 1, chans), 2), HEAD_DIM) == iota((HEADS, 1, chans), 0)
    own = head_of.astype(F32)
    for c in range(width):
        spread = (query[c][None] * own).reshape(stack, chans).astype(BF16)
        key = at_cell(far_keys, mid_keys, c)
        scores[c] = lax.dot_general(spread, key, NT, preferred_element_type=F32)
    flat = width * stack
    expo = jnp.exp(scores[...].reshape(flat, near) * HEAD_DIM ** (-0.5))

    def split_dot(a, dims):
        high = jnp.minimum(a, float(jnp.finfo(BF16).max)).astype(BF16)
        rest = (a - high.astype(F32)).astype(BF16)
        return lax.dot_general(high, member, dims, preferred_element_type=F32) + lax.dot_general(
            rest, member, dims, preferred_element_type=F32
        )

    sums = split_dot(expo, (((1,), (0,)), ((), ()))).reshape(width * HEADS, frames, LANES)
    frame_count = jnp.sum(cover, axis=2, keepdims=True)
    coef = (cover / (frame_count * jnp.where(cover > 0, sums, 1.0))).reshape(flat, LANES)
    back = split_dot(coef, NT)
    scores[...] = (expo * back).reshape(width, stack, near)
    for c in range(width):
        value = at_cell(far_values, mid_values, c)
        product = dot(scores[c].astype(BF16), value).reshape(HEADS, frames, chans)
        mixed[c] = jnp.sum(jnp.where(head_of, product, 0.0), axis=0)
    joined = mixed[...].reshape(width * frames, chans).astype(BF16)
    joined = dot(swap_matrix(frames, width, True), joined).astype(BF16)
    projected = dot(joined, out_w_ref[...])
    output = resid_ref[...].astype(F32) + projected + out_b_ref[...].reshape(1, chans)
    out_ref[...] = output.astype(BF16).reshape(frames, width, chans)


def passed(shard, by):
    size = lax.axis_size("frames")
    pairs = [(i, i + by) for i in range(size) if 0 <= i + by < size]
    return lax.ppermute(shard, "frames", pairs)


def on_device(
    video, window_gaps, gn_gain, gn_bias, conv_weight, conv_bias,
    ln_gain, ln_bias, qkv_weight, out_weight, out_bias,
):
    frames, _, width, chans = video.shape
    bands = lax.axis_size("height")
    place = lax.axis_index("height")
    outs = conv_weight.shape[1]
    cells = frames * width
    row = video.reshape(frames, width, chans)
    copies = jnp.broadcast_to(row[None], (bands, frames, width, chans))
    whole = lax.all_to_all(copies, "height", 0, 0, tiled=True)
    weight = lax.all_gather(conv_weight.T, "frames", axis=0, tiled=False)
    cbias = lax.dynamic_slice_in_dim(conv_bias, place * outs, outs)[None]
    parts = pl.pallas_call(
        conv_kernel,
        out_shape=jax.ShapeDtypeStruct((bands, outs, cells), BF16),
        in_specs=[VMEM] * 5,
        out_specs=VMEM,
        compiler_params=GRANT,
        scratch_shapes=[
            pltpu.VMEM((bands + 2, frames, width, chans), BF16),
            pltpu.VMEM((outs, 9 * chans), BF16),
        ],
    )(on_chip(whole), on_chip(weight), gn_gain, gn_bias, cbias)
    parts = lax.all_to_all(parts, "height", 0, 0, tiled=True)
    resid, norm = pl.pallas_call(
        norm_kernel,
        out_shape=[jax.ShapeDtypeStruct((cells, chans), BF16)] * 2,
        in_specs=[VMEM] * 4,
        out_specs=[VMEM] * 2,
        compiler_params=GRANT,
    )(on_chip(parts), row, ln_gain, ln_bias)
    b3, b1 = passed(norm, -1), passed(norm, 1)
    b4, b0 = passed(b3, -1), passed(norm, 2)
    qkv = on_chip(qkv_weight)
    own = jax.ShapeDtypeStruct((width, frames, chans), F32)
    mid = jax.ShapeDtypeStruct((3, width, frames, chans), F32)
    early = pl.pallas_call(
        early_kernel,
        out_shape=[jax.ShapeDtypeStruct((5 * frames, LANES), F32), own, mid, mid],
        in_specs=[SMEM] + [VMEM] * 4,
        out_specs=[VMEM] * 4,
        compiler_params=GRANT,
    )(window_gaps, on_chip(b1), norm, on_chip(b3), qkv)
    out = pl.pallas_call(
        attend_kernel,
        out_shape=jax.ShapeDtypeStruct((frames, width, chans), BF16),
        in_specs=[VMEM] * 10,
        out_specs=VMEM,
        compiler_params=GRANT,
        scratch_shapes=[
            pltpu.VMEM((2, width, frames, chans), F32),
            pltpu.VMEM((2, width, frames, chans), F32),
            pltpu.VMEM((width, HEADS * frames, 5 * frames), F32),
            pltpu.VMEM((width, frames, chans), F32),
        ],
    )(
        on_chip(b4), on_chip(b0), *[on_chip(n) for n in early], on_chip(resid), qkv,
        on_chip(out_weight), on_chip(out_bias),
    )
    return out.reshape(frames, 1, width, chans)


def solution(mesh):
    placed = (
        P(("dp", "frames"), "height", None, None),
        P("dp"),
        P(),
        P(),
        P("frames", "height"),
        P(),
        P(),
        P(),
        P(),
        P(),
        P(),
    )
    return jax.shard_map(
        on_device,
        mesh=mesh,
        in_specs=placed,
        out_specs=P(("dp", "frames"), "height", None, None),
        check_vma=False,
    )
```
